32 devices in a mesh: grp: 4 (over x, core), mem: 8 (over z, y).
Axes of the slice: x: 2, y: 2, z: 4, core: 2. Of those that a mesh axis runs over, the one named last changes fastest.
Arguments:
- features: bfloat16 [32768, 4096], P(('grp', 'mem')), may hold values from -0.09375 to 0.09375
- re_features: bfloat16 [32768, 256], P(('grp', 'mem')), may hold values from -6 to 6
- member_id: int32 [32768], P(('grp', 'mem')), may hold values from 0 to 255, as said below
- slot: int32 [32768], P(('grp', 'mem')), may hold values from 0 to 2047, as said below
- labels: int32 [32768], P(('grp', 'mem')), may hold values 0 or 1
- offsets: float32 [32768], P(('grp', 'mem')), may hold values from -6 to 6
- feature_scale: float32 [4096], replicated, may hold values from 0.3 to 3
- w_start: float32 [4096], replicated, may hold values from -4 to 4
Outputs:
- fixed_weights: float32 [4096], replicated
- member_coef: float32 [256, 256], P(('grp', 'mem'))
- row_offsets: float32 [32768], P(('grp', 'mem'))
The draws below stay inside these ranges and needn't reach their ends.
Inputs may be any that keep to these rules, and one draw needn't show every extreme that they name: A row of device k (devices counted along grp, then mem) belongs to group k // 8: member_id // 64 is that group, and (member_id mod 64) // 8 equals slot // 256. Rows per member are uneven. Within one device's rows the slots are distinct; slot // 256 is the mem index that owns the row's member, so at most 256 rows of one device go to one owner, and in every group one owner receives exactly 256 rows from every device of the group.
All inputs are finite; a program needn't handle non-finite values. No bound on the sum of `labels` on one device may be relied on, other than what follows from the above.
Results may differ from the reference program's by a relative error of at most 0.0003.
Values may be sent and summed in bfloat16 or wider, within the bound.
A program may use at most 64 MiB of HBM per device.

```python
import math
import jax
import jax.numpy as jnp
from jax import lax

F = 4096
FR = 256
ROWS_DEV = 1024
MEM_DEV = 8
NEWTON = 2
CG_ITERS = 3
ROWS = 32768
CAP = 256
SLOTS = 2048
GROUP_MEMBERS = 64
MEMBERS = 256
N_GRP = 4
N_MEM = 8


def layout_rows(key):
    base = jax.random.fold_in(key, 7001)

    def one_block(block_key, block):
        group = block // N_MEM
        group_key = jax.random.fold_in(base, 500000 + group)
        key_noise, key_rows, key_first, key_second = jax.random.split(block_key, 4)
        ranking = jax.random.permutation(group_key, N_MEM).astype(jnp.int32)
        owner_of = jnp.arange(SLOTS, dtype=jnp.int32) // CAP
        rank_of = ranking[owner_of]
        noise = jax.random.randint(key_noise, (SLOTS,), 0, 4096, dtype=jnp.int32)
        priority = jnp.where(rank_of == 0, noise - 4096, noise * (1 + rank_of))
        keyed = priority * SLOTS + jnp.arange(SLOTS, dtype=jnp.int32)
        picked = jnp.argsort(keyed)[:ROWS_DEV].astype(jnp.int32)
        shuffle = jax.random.permutation(key_rows, ROWS_DEV).astype(jnp.int32)
        slot_rows = picked[shuffle]
        local_id = jnp.minimum(jax.random.randint(key_first, (ROWS_DEV,), 0, MEM_DEV, dtype=jnp.int32), jax.random.randint(key_second, (ROWS_DEV,), 0, MEM_DEV, dtype=jnp.int32))
        member_rows = group * GROUP_MEMBERS + slot_rows // CAP * MEM_DEV + local_id
        return (member_rows.astype(jnp.int32), slot_rows)
    block_keys = jax.random.split(base, N_GRP * N_MEM)
    members, slots = jax.vmap(one_block)(block_keys, jnp.arange(N_GRP * N_MEM, dtype=jnp.int32))
    return (members.reshape(-1), slots.reshape(-1))


def draw_member_id(key, part):
    return layout_rows(key)[0]


def draw_slot(key, part):
    return layout_rows(key)[1]


def with_ends(values, rng, smallest, top_value):
    longest = values.shape.index(max(values.shape))
    spots = []
    for shift in (0, 1):
        where = [jax.random.randint(jax.random.fold_in(rng, axis), (), 0, length) for axis, length in enumerate(values.shape)]
        where[longest] = (where[longest] + shift) % values.shape[longest]
        spots.append(tuple(where))
    return values.at[spots[0]].set(smallest).at[spots[1]].set(top_value)


def levels(key, extent, pieces, low, top_value):
    level = 1.0
    for axis_at, shards_of in pieces:
        steps = jax.random.uniform(jax.random.fold_in(jax.random.fold_in(key, 6), axis_at), (shards_of,), jnp.float32, low / len(pieces), top_value / len(pieces))
        level = level * jnp.repeat(jnp.exp(steps), extent[axis_at] // shards_of).reshape((-1,) + (1,) * (len(extent) - 1 - axis_at))
    return level


def normal_values(rng, dims, scale, reach, cuts=(), held_as=jnp.bfloat16):
    gain = levels(rng, dims, cuts, -0.22, 0.18) if cuts else 1.0
    array = jax.random.normal(rng, dims, jnp.float32) * scale * gain
    return jnp.minimum(jnp.maximum(array, -reach), reach).astype(held_as)


def setup_inputs(seed: int = 0) -> dict:
    splits = jax.random.split(jax.random.key(seed), 9)
    return {
        "features": normal_values(splits[0], (ROWS, F), F ** -0.5, 0.09375, ((0, 32),)),
        "re_features": normal_values(splits[1], (ROWS, FR), 1.0, 6.0, ((0, 32),)),
        "member_id": draw_member_id(jax.random.fold_in(splits[8], 71), 0),
        "slot": draw_slot(jax.random.fold_in(splits[8], 71), 0),
        "labels": with_ends((jax.random.randint(splits[4], (ROWS,), 0, 2) < 1).astype(jnp.int32), jax.random.fold_in(splits[4], 1), 0, 1),
        "offsets": normal_values(splits[5], (ROWS,), 1.0, 6.0, ((0, 32),), jnp.float32),
        "feature_scale": jnp.clip(jnp.exp(jax.random.uniform(splits[6], (F,), jnp.float32, math.log(0.3), math.log(3.0))), 0.3, 3.0),
        "w_start": normal_values(splits[7], (F,), 0.5, 4.0, (), jnp.float32),
    }


ridge_fixed = 1.0
ridge_member = 1.0

def split_pair(values):
    upper_part = values.astype(jnp.bfloat16)
    held_part = lax.optimization_barrier(upper_part)
    lower_part = (values - held_part.astype(jnp.float32)).astype(jnp.bfloat16)
    return (upper_part, lower_part)

def split_two(vector):
    upper_part, lower_part = split_pair(vector)
    return jnp.stack([upper_part, lower_part], axis=1)

def apply_rows(features, vector):
    return jnp.sum(jnp.dot(features.astype(jnp.float32), split_two(vector).astype(jnp.float32), preferred_element_type=jnp.float32), axis=1)

def apply_columns(features, values):
    pair_cols = split_two(values)
    product = lax.dot_general(pair_cols.astype(jnp.float32), features.astype(jnp.float32), (((0,), (0,)), ((), ())), preferred_element_type=jnp.float32)
    return jnp.sum(product, axis=0)

def inner_rows(left, right):
    return lax.dot_general(left.astype(jnp.float32), right.astype(jnp.float32), (((0,), (0,)), ((), ())), preferred_element_type=jnp.float32)

def fit_members(received, arrived):
    curv_row = arrived[0]
    resid_row = arrived[1]
    local_row = arrived[2]
    onehot = (local_row[:, None] == jnp.arange(MEM_DEV).astype(arrived.dtype)[None, :]).astype(arrived.dtype)
    z_float = received.astype(jnp.float32)

    def gram_one(column):
        upper_part, lower_part = split_pair(z_float * (curv_row * column)[:, None])
        return inner_rows(received, upper_part) + inner_rows(received, lower_part)
    gram_all = lax.map(gram_one, onehot.T) + ridge_member * jnp.eye(received.shape[1], dtype=jnp.float32)
    grad_upper, grad_lower = split_pair(resid_row[:, None] * onehot)
    member_grad = inner_rows(grad_upper, received) + inner_rows(grad_lower, received)
    factor = jnp.linalg.cholesky(gram_all)
    member_coef = -jax.scipy.linalg.cho_solve((factor, True), member_grad[:, :, None])[:, :, 0]
    coef_upper, coef_lower = split_pair(member_coef)
    scores = jnp.dot(received.astype(jnp.float32), coef_upper.T.astype(jnp.float32), preferred_element_type=jnp.float32) + jnp.dot(received.astype(jnp.float32), coef_lower.T.astype(jnp.float32), preferred_element_type=jnp.float32)
    return (member_coef, jnp.sum(scores * onehot, axis=1))

def reference(features, re_features, member_id, slot, labels, offsets, feature_scale, w_start):
    target = labels.astype(jnp.float32)
    weights = w_start
    for newton_step in range(NEWTON):
        margin = apply_rows(features, feature_scale * weights) + offsets
        probability = jax.nn.sigmoid(margin)
        curvature = probability * (1.0 - probability)
        gradient = feature_scale * apply_columns(features, probability - target) + ridge_fixed * weights
        residual = -gradient
        direction = residual
        res_norm = jnp.sum(residual * residual)
        update = jnp.zeros_like(weights)
        for cg_step in range(CG_ITERS):
            inner = curvature * apply_rows(features, feature_scale * direction)
            hess_image = feature_scale * apply_columns(features, inner) + ridge_fixed * direction
            step_size = res_norm / jnp.sum(direction * hess_image)
            update = update + step_size * direction
            residual = residual - step_size * hess_image
            next_norm = jnp.sum(residual * residual)
            direction = residual + next_norm / res_norm * direction
            res_norm = next_norm
        weights = weights + update
    score = apply_rows(features, feature_scale * weights)
    probability = jax.nn.sigmoid(score)
    curvature = probability * (1.0 - probability)
    resid_row = probability - target
    local_id = (member_id % MEM_DEV).astype(jnp.float32)
    row_weights = jnp.stack([curvature, resid_row, local_id], axis=1)
    device_of = (jnp.arange(ROWS, dtype=jnp.int32) // ROWS_DEV).astype(jnp.int32)
    flat_slot = (device_of * SLOTS + slot).astype(jnp.int32)
    owners_all = N_GRP * N_MEM
    z_buffer = jnp.zeros((owners_all * SLOTS, FR), re_features.dtype).at[flat_slot].set(re_features)
    w_buffer = jnp.zeros((owners_all * SLOTS, 3), jnp.float32).at[flat_slot].set(row_weights)
    z_owner = z_buffer.reshape(N_GRP, N_MEM, N_MEM, CAP, FR).transpose(0, 2, 1, 3, 4).reshape(owners_all, SLOTS, FR)
    w_owner = w_buffer.reshape(N_GRP, N_MEM, N_MEM, CAP, 3).transpose(0, 2, 1, 3, 4).reshape(owners_all, SLOTS, 3)
    all_coef, slot_scores = lax.map(lambda pair_in: fit_members(pair_in[0], pair_in[1].T), (z_owner, w_owner))
    back_flat = slot_scores.reshape(N_GRP, N_MEM, N_MEM, CAP).transpose(0, 2, 1, 3).reshape(-1)
    row_offsets = back_flat[flat_slot]
    return (weights, all_coef.reshape(MEMBERS, FR), row_offsets)
```

```python
import functools

import jax
import jax.numpy as jnp
from jax import lax
from jax.experimental import pallas as pl
from jax.experimental.pallas import tpu as pltpu
from jax.sharding import PartitionSpec as P

MEM_DEV = 8
NEWTON = 2
CG_ITERS = 3
LANES = 128
BLOCK = 32

ridge_fixed = 1.0
ridge_member = 1.0
MESH_ID = pl.DeviceIdType.MESH
NT = (((1,), (1,)), ((), ()))
NN = (((1,), (0,)), ((), ()))
TN = (((0,), (0,)), ((), ()))


def pair_rows(row):
    upper = row.astype(jnp.bfloat16).astype(jnp.float32)
    lower = (row - upper).astype(jnp.bfloat16).astype(jnp.float32)
    at = lax.broadcasted_iota(jnp.int32, (16, row.shape[1]), 0)
    both = jnp.where(at == 0, upper, jnp.where(at == 1, lower, 0.0))
    return both.astype(jnp.bfloat16)


def fit_kernel(
    n_grp, n_mem,
    feat, label_ref, offset_ref, scale_ref, start_ref,
    weight_ref, curv_ref, resid_ref,
    vec_w, vec_u, vec_r, vec_p, curv, send, recv, send_sem, recv_sem,
):
    rows, width = feat.shape
    lines = width // LANES
    me_grp = lax.axis_index("grp")
    me_mem = lax.axis_index("mem")

    partners = []
    for name, me, size in (("mem", me_mem, n_mem), ("grp", me_grp, n_grp)):
        bit = 1
        while bit < size:
            other = me + bit * (1 - 2 * ((me // bit) % 2))
            partners.append(
                (me_grp, other) if name == "mem" else (other, me_mem)
            )
            bit *= 2

    barrier = pltpu.get_barrier_semaphore()
    for partner in partners:
        pl.semaphore_signal(barrier, inc=1, device_id=partner, device_id_type=MESH_ID)
    pl.semaphore_wait(barrier, len(partners))

    def all_sum(value, call):
        for step, partner in enumerate(partners):
            send[call, step] = value
            copy = pltpu.make_async_remote_copy(
                src_ref=send.at[call, step],
                dst_ref=recv.at[call, step],
                send_sem=send_sem.at[call, step],
                recv_sem=recv_sem.at[call, step],
                device_id=partner,
                device_id_type=MESH_ID,
            )
            copy.start()
            copy.wait()
            value = value + recv[call, step]
        return value

    def times_rows(vector):
        row = jnp.concatenate([vector[i : i + 1, :] for i in range(lines)], axis=1)
        pair = pair_rows(row)
        parts = []
        for first in range(0, rows, 256):
            got = lax.dot_general(
                pair, feat[first : first + 256, :], NT, preferred_element_type=jnp.float32
            )
            parts.append(got[0:1] + got[1:2])
        return jnp.concatenate(parts, axis=1)

    def times_columns(row):
        pair = pair_rows(row)
        parts = []
        for first in range(0, width, 256):
            got = lax.dot_general(
                pair, feat[:, first : first + 256], NN, preferred_element_type=jnp.float32
            )
            got = got[0:1] + got[1:2]
            parts += [got[:, at : at + LANES] for at in range(0, 256, LANES)]
        return jnp.concatenate(parts, axis=0)

    def total(value):
        return jnp.sum(jnp.sum(value, axis=1, keepdims=True), axis=0, keepdims=True)

    scale = scale_ref[...]
    target = label_ref[...].astype(jnp.float32)
    vec_w[...] = start_ref[...]

    def newton(step, carry):
        base = step * (CG_ITERS + 1)
        weights = vec_w[...]
        margin = times_rows(scale * weights) + offset_ref[...]
        prob = 1.0 / (1.0 + jnp.exp(-margin))
        curv[...] = prob * (1.0 - prob)
        summed = all_sum(times_columns(prob - target), base)
        resid = -(scale * summed + ridge_fixed * weights)
        vec_r[...] = resid
        vec_p[...] = resid
        vec_u[...] = jnp.zeros_like(resid)

        def cg(k, norm):
            direction = vec_p[...]
            inner = curv[...] * times_rows(scale * direction)
            image = scale * all_sum(times_columns(inner), base + 1 + k) + ridge_fixed * direction
            size = norm / total(direction * image)
            vec_u[...] = vec_u[...] + size * direction
            left = vec_r[...] - size * image
            vec_r[...] = left
            new_norm = total(left * left)
            vec_p[...] = left + new_norm / norm * direction
            return new_norm

        lax.fori_loop(0, CG_ITERS, cg, total(resid * resid))
        vec_w[...] = weights + vec_u[...]
        return carry

    lax.fori_loop(0, NEWTON, newton, 0)
    weights = vec_w[...]
    weight_ref[...] = weights
    score = times_rows(scale * weights)
    prob = 1.0 / (1.0 + jnp.exp(-score))
    curv_ref[...] = prob * (1.0 - prob)
    resid_ref[...] = prob - target


def fit_fixed(features, labels, offsets, feature_scale, w_start, n_grp, n_mem):
    rows, width = features.shape
    lines = width // LANES
    steps = (n_grp.bit_length() - 1) + (n_mem.bit_length() - 1)
    calls = NEWTON * (CG_ITERS + 1)
    line = jax.ShapeDtypeStruct((lines, LANES), jnp.float32)
    row = jax.ShapeDtypeStruct((1, rows), jnp.float32)
    held = pltpu.VMEM((lines, LANES), jnp.float32)
    whole = pl.BlockSpec(memory_space=pltpu.VMEM)
    return pl.pallas_call(
        functools.partial(fit_kernel, n_grp, n_mem),
        out_shape=(line, row, row),
        in_specs=[whole] * 5,
        out_specs=(whole,) * 3,
        scratch_shapes=[
            held, held, held, held,
            pltpu.VMEM((1, rows), jnp.float32),
            pltpu.VMEM((calls, steps, lines, LANES), jnp.float32),
            pltpu.VMEM((calls, steps, lines, LANES), jnp.float32),
            pltpu.SemaphoreType.DMA((calls, steps)),
            pltpu.SemaphoreType.DMA((calls, steps)),
        ],
        compiler_params=pltpu.CompilerParams(
            collective_id=0, has_side_effects=True, vmem_limit_bytes=40 << 20
        ),
        name="fit_fixed",
    )(
        features,
        labels.reshape(1, rows),
        offsets.reshape(1, rows),
        feature_scale.reshape(lines, LANES),
        w_start.reshape(lines, LANES),
    )


def three_parts(value):
    first = value.astype(jnp.bfloat16)
    rest = value - first.astype(jnp.float32)
    second = rest.astype(jnp.bfloat16)
    third = (rest - second.astype(jnp.float32)).astype(jnp.bfloat16)
    return first, second, third


def invert_blocks(blocks):
    lane = lax.broadcasted_iota(jnp.int32, (BLOCK, LANES), 1)
    sub = lax.broadcasted_iota(jnp.int32, (BLOCK, LANES), 0)
    base = lane // BLOCK * BLOCK
    place = lane % BLOCK
    for k in range(BLOCK):
        here = place == k
        new = []
        for value in blocks:
            column = jnp.take_along_axis(value, base + k, axis=1)
            pivot = 1.0 / column[k : k + 1, :]
            row = jnp.where(here[k : k + 1, :], pivot, value[k : k + 1, :] * pivot)
            value = jnp.where(here, 0.0, value) - column * row
            new.append(jnp.where(sub == k, row, value))
        blocks = new
    return blocks


def member_kernel(z_ref, zt_ref, curv_ref, resid_ref, local_ref, coef_ref, score_ref, gram, upper, lower):
    width = z_ref.shape[1]
    slots = z_ref.shape[0]
    count = coef_ref.shape[0]
    per = LANES // BLOCK
    blocks = width // BLOCK
    local = local_ref[...]
    weighted = zt_ref[...].astype(jnp.float32) * curv_ref[...]
    first = weighted.astype(jnp.bfloat16)
    upper[...] = first
    lower[...] = (weighted - first.astype(jnp.float32)).astype(jnp.bfloat16)
    eye = (
        lax.broadcasted_iota(jnp.int32, (width, width), 0)
        == lax.broadcasted_iota(jnp.int32, (width, width), 1)
    ).astype(jnp.float32)

    @pl.loop(0, count)
    def _(m):
        mask = jnp.where(local == m.astype(jnp.float32), 1.0, 0.0).astype(jnp.bfloat16)
        total = lax.dot_general(
            upper[...] * mask, z_ref[...], NN, preferred_element_type=jnp.float32
        ) + lax.dot_general(
            lower[...] * mask, z_ref[...], NN, preferred_element_type=jnp.float32
        )
        gram[m] = total + ridge_member * eye

    member = lax.broadcasted_iota(jnp.int32, (count, slots), 0).astype(jnp.float32)
    own = member == local
    masked = jnp.where(own, resid_ref[...], 0.0)
    high = masked.astype(jnp.bfloat16)
    low = (masked - high.astype(jnp.float32)).astype(jnp.bfloat16)
    grad = lax.dot_general(
        high, z_ref[...], NN, preferred_element_type=jnp.float32
    ) + lax.dot_general(low, z_ref[...], NN, preferred_element_type=jnp.float32)
    rhs = [grad[m : m + 1, :] for m in range(count)]
    exact = dict(preferred_element_type=jnp.float32, precision=lax.Precision.HIGHEST)
    inverse_of = []
    heads = {}
    for b in range(blocks):
        lo, hi = b * BLOCK, (b + 1) * BLOCK
        squares = [gram[m, lo:hi, lo:hi] for m in range(count)]
        packed = [
            jnp.concatenate(squares[at : at + per], axis=1) for at in range(0, count, per)
        ]
        packed = invert_blocks(packed)
        inverses = [
            packed[m // per][:, m % per * BLOCK : (m % per + 1) * BLOCK] for m in range(count)
        ]
        panels = []
        if hi < width:
            for m in range(count):
                right = gram[m, lo:hi, hi:width]
                panel = lax.dot_general(inverses[m], right, NN, **exact)
                panels.append(panel)
                a1, a2, a3 = three_parts(right)
                b1, b2, b3 = three_parts(panel)
                left_cat = jnp.concatenate([a1, a1, a2, a2, a1, a3], axis=0)
                right_cat = jnp.concatenate([b1, b2, b1, b2, b3, b1], axis=0)
                gram[m, hi:width, hi:width] = gram[m, hi:width, hi:width] - lax.dot_general(
                    left_cat, right_cat, TN, preferred_element_type=jnp.float32
                )
                now = rhs[m]
                heads[(m, b)] = now[:, :BLOCK]
                rhs[m] = now[:, BLOCK:] - lax.dot_general(now[:, :BLOCK], panel, NN, **exact)
        else:
            for m in range(count):
                heads[(m, b)] = rhs[m]
        inverse_of.append((inverses, panels))
    solved = []
    for m in range(count):
        tail = None
        for b in reversed(range(blocks)):
            inverses, panels = inverse_of[b]
            part = lax.dot_general(heads[(m, b)], inverses[m], NN, **exact)
            if tail is not None:
                part = part - lax.dot_general(tail, panels[m], NT, **exact)
                tail = jnp.concatenate([part, tail], axis=1)
            else:
                tail = part
        solved.append(tail)
    coef = -jnp.concatenate(solved, axis=0)
    coef_ref[...] = coef
    high = coef.astype(jnp.bfloat16)
    low = (coef - high.astype(jnp.float32)).astype(jnp.bfloat16)
    scores = lax.dot_general(
        high, zt_ref[...], NN, preferred_element_type=jnp.float32
    ) + lax.dot_general(low, zt_ref[...], NN, preferred_element_type=jnp.float32)
    score_ref[...] = jnp.sum(jnp.where(own, scores, 0.0), axis=0, keepdims=True)


def fit_members(received, curv, resid, local):
    slots, width = received.shape
    whole = pl.BlockSpec(memory_space=pltpu.VMEM)
    return pl.pallas_call(
        member_kernel,
        out_shape=(
            jax.ShapeDtypeStruct((MEM_DEV, width), jnp.float32),
            jax.ShapeDtypeStruct((1, slots), jnp.float32),
        ),
        in_specs=[whole] * 5,
        out_specs=(whole,) * 2,
        scratch_shapes=[
            pltpu.VMEM((MEM_DEV, width, width), jnp.float32),
            pltpu.VMEM((width, slots), jnp.bfloat16),
            pltpu.VMEM((width, slots), jnp.bfloat16),
        ],
        compiler_params=pltpu.CompilerParams(vmem_limit_bytes=48 << 20),
        name="fit_members",
    )(received, received.T, curv, resid, local)


def on_device(n_grp, n_mem, features, re_features, member_id, slot, labels, offsets, feature_scale, w_start):
    row_count = features.shape[0]
    slots_all = 2 * row_count
    packed = jnp.zeros((slots_all, re_features.shape[1]), jnp.bfloat16).at[slot].set(re_features)
    received = lax.all_to_all(packed, "mem", split_axis=0, concat_axis=0, tiled=True)
    weights, curvature, resid_row = fit_fixed(
        features, labels, offsets, feature_scale, w_start, n_grp, n_mem
    )
    local_id = (member_id % MEM_DEV).astype(jnp.float32)
    row_weights = jnp.concatenate([curvature, resid_row, local_id[None, :]], axis=0)
    weight_slots = jnp.zeros((3, slots_all), jnp.float32).at[:, slot].set(row_weights)
    arrived = lax.all_to_all(weight_slots, "mem", split_axis=1, concat_axis=1, tiled=True)
    member_coef, slot_scores = fit_members(received, arrived[0:1], arrived[1:2], arrived[2:3])
    returned = lax.all_to_all(slot_scores[0], "mem", split_axis=0, concat_axis=0, tiled=True)
    row_offsets = returned[slot]
    return (weights.reshape(-1), member_coef, row_offsets)


def solution(mesh):
    placed = (
        P(("grp", "mem"), None),
        P(("grp", "mem"), None),
        P(("grp", "mem")),
        P(("grp", "mem")),
        P(("grp", "mem")),
        P(("grp", "mem")),
        P(),
        P(),
    )
    return jax.shard_map(
        functools.partial(on_device, mesh.shape["grp"], mesh.shape["mem"]),
        mesh=mesh,
        in_specs=placed,
        out_specs=(P(), P(("grp", "mem"), None), P(("grp", "mem"))),
        check_vma=False,
    )
```

```python
import functools

import jax
import jax.numpy as jnp
from jax import lax
from jax.experimental import pallas as pl
from jax.experimental.pallas import tpu as pltpu
from jax.sharding import PartitionSpec as P

MEM_DEV = 8
NEWTON = 2
CG_ITERS = 3
LANES = 128
BLOCK = 32

ridge_fixed = 1.0
ridge_member = 1.0
MESH_ID = pl.DeviceIdType.MESH
NT = (((1,), (1,)), ((), ()))
NN = (((1,), (0,)), ((), ()))
TN = (((0,), (0,)), ((), ()))


def pair_rows(row):
    upper = row.astype(jnp.bfloat16).astype(jnp.float32)
    lower = (row - upper).astype(jnp.bfloat16).astype(jnp.float32)
    at = lax.broadcasted_iota(jnp.int32, (16, row.shape[1]), 0)
    both = jnp.where(at == 0, upper, jnp.where(at == 1, lower, 0.0))
    return both.astype(jnp.bfloat16)


def three_parts(value):
    first = value.astype(jnp.bfloat16)
    rest = value - first.astype(jnp.float32)
    second = rest.astype(jnp.bfloat16)
    third = (rest - second.astype(jnp.float32)).astype(jnp.bfloat16)
    return first, second, third


def invert_blocks(blocks):
    lane = lax.broadcasted_iota(jnp.int32, (BLOCK, LANES), 1)
    sub = lax.broadcasted_iota(jnp.int32, (BLOCK, LANES), 0)
    base = lane // BLOCK * BLOCK
    place = lane % BLOCK
    for k in range(BLOCK):
        here = place == k
        new = []
        for value in blocks:
            column = jnp.take_along_axis(value, base + k, axis=1)
            pivot = 1.0 / column[k : k + 1, :]
            row = jnp.where(here[k : k + 1, :], pivot, value[k : k + 1, :] * pivot)
            value = jnp.where(here, 0.0, value) - column * row
            new.append(jnp.where(sub == k, row, value))
        blocks = new
    return blocks


def fit_members(z_ref, zt_ref, curv_row, resid_row, local, coef_ref, gram, upper, lower):
    width = z_ref.shape[1]
    slots = z_ref.shape[0]
    count = coef_ref.shape[0]
    per = LANES // BLOCK
    blocks = width // BLOCK
    weighted = zt_ref[...].astype(jnp.float32) * curv_row
    first = weighted.astype(jnp.bfloat16)
    upper[...] = first
    lower[...] = (weighted - first.astype(jnp.float32)).astype(jnp.bfloat16)
    eye = (
        lax.broadcasted_iota(jnp.int32, (width, width), 0)
        == lax.broadcasted_iota(jnp.int32, (width, width), 1)
    ).astype(jnp.float32)

    @pl.loop(0, count)
    def _(m):
        mask = jnp.where(local == m.astype(jnp.float32), 1.0, 0.0).astype(jnp.bfloat16)
        total = lax.dot_general(
            upper[...] * mask, z_ref[...], NN, preferred_element_type=jnp.float32
        ) + lax.dot_general(
            lower[...] * mask, z_ref[...], NN, preferred_element_type=jnp.float32
        )
        gram[m] = total + ridge_member * eye

    member = lax.broadcasted_iota(jnp.int32, (count, slots), 0).astype(jnp.float32)
    own = member == local
    masked = jnp.where(own, resid_row, 0.0)
    high = masked.astype(jnp.bfloat16)
    low = (masked - high.astype(jnp.float32)).astype(jnp.bfloat16)
    grad = lax.dot_general(
        high, z_ref[...], NN, preferred_element_type=jnp.float32
    ) + lax.dot_general(low, z_ref[...], NN, preferred_element_type=jnp.float32)
    rhs = [grad[m : m + 1, :] for m in range(count)]
    exact = dict(preferred_element_type=jnp.float32, precision=lax.Precision.HIGHEST)
    inverse_of = []
    heads = {}
    for b in range(blocks):
        lo, hi = b * BLOCK, (b + 1) * BLOCK
        squares = [gram[m, lo:hi, lo:hi] for m in range(count)]
        packed = [
            jnp.concatenate(squares[at : at + per], axis=1) for at in range(0, count, per)
        ]
        packed = invert_blocks(packed)
        inverses = [
            packed[m // per][:, m % per * BLOCK : (m % per + 1) * BLOCK] for m in range(count)
        ]
        panels = []
        if hi < width:
            for m in range(count):
                right = gram[m, lo:hi, hi:width]
                panel = lax.dot_general(inverses[m], right, NN, **exact)
                panels.append(panel)
                a1, a2, a3 = three_parts(right)
                b1, b2, b3 = three_parts(panel)
                left_cat = jnp.concatenate([a1, a1, a2, a2, a1, a3], axis=0)
                right_cat = jnp.concatenate([b1, b2, b1, b2, b3, b1], axis=0)
                gram[m, hi:width, hi:width] = gram[m, hi:width, hi:width] - lax.dot_general(
                    left_cat, right_cat, TN, preferred_element_type=jnp.float32
                )
                now = rhs[m]
                heads[(m, b)] = now[:, :BLOCK]
                rhs[m] = now[:, BLOCK:] - lax.dot_general(now[:, :BLOCK], panel, NN, **exact)
        else:
            for m in range(count):
                heads[(m, b)] = rhs[m]
        inverse_of.append((inverses, panels))
    solved = []
    for m in range(count):
        tail = None
        for b in reversed(range(blocks)):
            inverses, panels = inverse_of[b]
            part = lax.dot_general(heads[(m, b)], inverses[m], NN, **exact)
            if tail is not None:
                part = part - lax.dot_general(tail, panels[m], NT, **exact)
                tail = jnp.concatenate([part, tail], axis=1)
            else:
                tail = part
        solved.append(tail)
    coef = -jnp.concatenate(solved, axis=0)
    coef_ref[...] = coef
    high = coef.astype(jnp.bfloat16)
    low = (coef - high.astype(jnp.float32)).astype(jnp.bfloat16)
    scores = lax.dot_general(
        high, zt_ref[...], NN, preferred_element_type=jnp.float32
    ) + lax.dot_general(low, zt_ref[...], NN, preferred_element_type=jnp.float32)
    return jnp.sum(jnp.where(own, scores, 0.0), axis=0, keepdims=True)


def window_kernel(
    n_grp, n_mem,
    feat_hbm, re_hbm, member_hbm, slot_hbm, label_hbm, offset_hbm, scale_hbm, start_hbm,
    weight_ref, coef_ref, offsets_ref,
    feat, re_ref, member_ref, slot_ref, label_ref, offset_ref, scale_ref, vec_w,
    vec_u, vec_r, vec_p, curv, send, recv,
    pick, z_send, z_ref, zs_ref, zt_ref, w_send, w_recv, s_send, s_recv, gram, upper, lower, row_vals,
    load_sem, feat_sem, send_sem, recv_sem, zs_sem, zr_sem, ws_sem, wr_sem, ss_sem, sr_sem,
):
    rows, width = feat.shape
    lines = width // LANES
    slots = z_ref.shape[0]
    cap = slots // n_mem
    calls = NEWTON * (CG_ITERS + 1)
    each = n_mem // calls
    me_grp = lax.axis_index("grp")
    me_mem = lax.axis_index("mem")

    loads = [
        pltpu.make_async_copy(source, target, load_sem.at[i])
        for i, (source, target) in enumerate(
            (
                (scale_hbm, scale_ref), (start_hbm, vec_w), (offset_hbm, offset_ref),
                (label_hbm, label_ref), (slot_hbm, slot_ref), (member_hbm, member_ref),
                (re_hbm, re_ref),
            )
        )
    ]
    feat_loads = [
        pltpu.make_async_copy(
            feat_hbm.at[pl.ds(first, 256)], feat.at[pl.ds(first, 256)], feat_sem.at[first // 256]
        )
        for first in range(0, rows, 256)
    ]
    for load in loads[:4] + feat_loads + loads[4:]:
        load.start()

    partners = []
    for name, me, size in (("mem", me_mem, n_mem), ("grp", me_grp, n_grp)):
        bit = 1
        while bit < size:
            other = me + bit * (1 - 2 * ((me // bit) % 2))
            partners.append((me_grp, other) if name == "mem" else (other, me_mem))
            bit *= 2

    barrier = pltpu.get_barrier_semaphore()
    for turn in range(1, n_mem):
        pl.semaphore_signal(
            barrier, inc=1, device_id=(me_grp, lax.rem(me_mem + turn, n_mem)), device_id_type=MESH_ID
        )
    for partner in partners[n_mem.bit_length() - 1 :]:
        pl.semaphore_signal(barrier, inc=1, device_id=partner, device_id_type=MESH_ID)
    pl.semaphore_wait(barrier, n_mem - 1 + n_grp.bit_length() - 1)
    for load in loads[:4]:
        load.wait()

    def peer(turn):
        return (me_grp, lax.rem(me_mem + turn, n_mem))

    def z_copy(turn):
        return pltpu.make_async_remote_copy(
            src_ref=z_send.at[turn - 1],
            dst_ref=z_ref.at[pl.ds(pl.multiple_of(me_mem * cap, cap), cap)],
            send_sem=zs_sem.at[turn - 1],
            recv_sem=zr_sem.at[turn - 1],
            device_id=peer(turn),
            device_id_type=MESH_ID,
        )

    def build(turn):
        first = pl.multiple_of(lax.rem(me_mem + turn, n_mem) * cap, cap)
        at = lax.broadcasted_iota(jnp.int32, (cap, rows), 0) + first
        chosen = jnp.where(at == slot_ref[...], 1.0, 0.0).astype(jnp.bfloat16)
        pick[pl.ds(first, cap), :] = chosen
        block = lax.dot_general(chosen, re_ref[...], NN, preferred_element_type=jnp.float32)
        block = block.astype(jnp.bfloat16)

        @pl.when(turn < n_mem)
        def _():
            z_send[turn - 1] = block

        @pl.when(turn == n_mem)
        def _():
            z_ref[pl.ds(pl.multiple_of(me_mem * cap, cap), cap), :] = block

    def all_sum(value, call):
        for step, partner in enumerate(partners):
            send[call, step] = value
            copy = pltpu.make_async_remote_copy(
                src_ref=send.at[call, step],
                dst_ref=recv.at[call, step],
                send_sem=send_sem.at[call, step],
                recv_sem=recv_sem.at[call, step],
                device_id=partner,
                device_id_type=MESH_ID,
            )
            copy.start()
            if step == 0:
                for q in range(each):
                    build(1 + call * each + q)
            copy.wait()
            value = value + recv[call, step]
        for q in range(each):
            turn = 1 + call * each + q

            @pl.when(turn < n_mem)
            def _():
                z_copy(turn).start()

        return value

    def times_rows(vector, loading=None):
        row = jnp.concatenate([vector[i : i + 1, :] for i in range(lines)], axis=1)
        pair = pair_rows(row)
        parts = []
        for first in range(0, rows, 256):
            if loading is not None:
                @pl.when(loading == 0)
                def _():
                    feat_loads[first // 256].wait()
            got = lax.dot_general(
                pair, feat[first : first + 256, :], NT, preferred_element_type=jnp.float32
            )
            parts.append(got[0:1] + got[1:2])
        return jnp.concatenate(parts, axis=1)

    def times_columns(row):
        pair = pair_rows(row)
        parts = []
        for first in range(0, width, 256):
            got = lax.dot_general(
                pair, feat[:, first : first + 256], NN, preferred_element_type=jnp.float32
            )
            got = got[0:1] + got[1:2]
            parts += [got[:, at : at + LANES] for at in range(0, 256, LANES)]
        return jnp.concatenate(parts, axis=0)

    def total(value):
        return jnp.sum(jnp.sum(value, axis=1, keepdims=True), axis=0, keepdims=True)

    scale = scale_ref[...]
    target = label_ref[...].astype(jnp.float32)

    def newton(step, carry):
        base = step * (CG_ITERS + 1)
        weights = vec_w[...]
        margin = times_rows(scale * weights, step) + offset_ref[...]
        prob = 1.0 / (1.0 + jnp.exp(-margin))
        curv[...] = prob * (1.0 - prob)
        grad = times_columns(prob - target)

        @pl.when(step == 0)
        def _():
            for load in loads[4:]:
                load.wait()

        summed = all_sum(grad, base)
        resid = -(scale * summed + ridge_fixed * weights)
        vec_r[...] = resid
        vec_p[...] = resid
        vec_u[...] = jnp.zeros_like(resid)

        def cg(k, norm):
            direction = vec_p[...]
            inner = curv[...] * times_rows(scale * direction)
            image = scale * all_sum(times_columns(inner), base + 1 + k) + ridge_fixed * direction
            size = norm / total(direction * image)
            vec_u[...] = vec_u[...] + size * direction
            left = vec_r[...] - size * image
            vec_r[...] = left
            new_norm = total(left * left)
            vec_p[...] = left + new_norm / norm * direction
            return new_norm

        lax.fori_loop(0, CG_ITERS, cg, total(resid * resid))
        vec_w[...] = weights + vec_u[...]
        return carry

    lax.fori_loop(0, NEWTON, newton, 0)
    weights = vec_w[...]
    weight_ref[...] = weights
    score = times_rows(scale * weights)
    prob = 1.0 / (1.0 + jnp.exp(-score))
    local_id = lax.rem(member_ref[...], MEM_DEV).astype(jnp.float32)
    row_vals[...] = jnp.zeros_like(row_vals)
    row_vals[0:1, :] = prob * (1.0 - prob)
    row_vals[1:2, :] = prob - target
    row_vals[2:3, :] = local_id
    parts = jnp.concatenate([p.astype(jnp.float32) for p in three_parts(row_vals[...])], axis=0)
    parts = jnp.concatenate([parts, jnp.zeros_like(parts[0:8])], axis=0).astype(jnp.bfloat16)

    def small_copy(source, target, turn, sends, recvs):
        return pltpu.make_async_remote_copy(
            src_ref=source.at[turn - 1],
            dst_ref=target.at[turn - 1],
            send_sem=sends.at[turn - 1],
            recv_sem=recvs.at[turn - 1],
            device_id=peer(turn),
            device_id_type=MESH_ID,
        )

    for turn in range(1, n_mem + 1):
        first = pl.multiple_of(lax.rem(me_mem + turn, n_mem) * cap, cap)
        got = lax.dot_general(
            parts, pick[pl.ds(first, cap), :], NT, preferred_element_type=jnp.float32
        )
        got = got[0:8] + got[8:16] + got[16:24]
        if turn < n_mem:
            w_send[turn - 1] = got
            small_copy(w_send, w_recv, turn, ws_sem, wr_sem).start()
        else:
            w_recv[n_mem - 1] = got
    for turn in range(1, n_mem):
        z_copy(turn).wait()
    for turn in range(1, n_mem + 1):
        source = lax.rem(me_mem + n_mem - turn, n_mem)
        block = z_ref[pl.ds(pl.multiple_of(source * cap, cap), cap), :]
        zt_ref[:, (turn - 1) * cap : turn * cap] = block.T
        zs_ref[(turn - 1) * cap : turn * cap, :] = block
    for turn in range(1, n_mem):
        small_copy(w_send, w_recv, turn, ws_sem, wr_sem).wait()
    arrived = jnp.concatenate([w_recv[t] for t in range(n_mem)], axis=1)
    scores = fit_members(
        zs_ref, zt_ref, arrived[0:1], arrived[1:2], arrived[2:3], coef_ref, gram, upper, lower
    )
    for turn in range(1, n_mem + 1):
        back = jnp.broadcast_to(scores[:, (turn - 1) * cap : turn * cap], (8, cap))
        if turn < n_mem:
            s_send[n_mem - turn - 1] = back
        else:
            s_recv[n_mem - 1] = back
    for turn in range(1, n_mem):
        small_copy(s_send, s_recv, turn, ss_sem, sr_sem).start()
    for turn in range(1, n_mem):
        small_copy(s_send, s_recv, turn, ss_sem, sr_sem).wait()
    result = jnp.zeros((1, rows), jnp.float32)
    for turn in range(1, n_mem + 1):
        owner = lax.rem(me_mem + n_mem - turn, n_mem)
        value = s_recv[turn - 1][0:1]
        p1, p2, p3 = (p.astype(jnp.float32) for p in three_parts(value))
        at = lax.broadcasted_iota(jnp.int32, (16, cap), 0)
        stack = jnp.where(at == 0, p1, jnp.where(at == 1, p2, jnp.where(at == 2, p3, 0.0)))
        got = lax.dot_general(
            stack.astype(jnp.bfloat16),
            pick[pl.ds(pl.multiple_of(owner * cap, cap), cap), :],
            NN,
            preferred_element_type=jnp.float32,
        )
        result = result + (got[0:1] + got[1:2] + got[2:3])
    offsets_ref[...] = result


def on_device(n_grp, n_mem, features, re_features, member_id, slot, labels, offsets, feature_scale, w_start):
    rows, width = features.shape
    inner = re_features.shape[1]
    lines = width // LANES
    slots = 2 * rows
    cap = slots // n_mem
    steps = (n_grp.bit_length() - 1) + (n_mem.bit_length() - 1)
    calls = NEWTON * (CG_ITERS + 1)
    f32, bf16, i32 = jnp.float32, jnp.bfloat16, jnp.int32
    held = pltpu.VMEM((lines, LANES), f32)
    dma = pltpu.SemaphoreType.DMA
    whole = pl.BlockSpec(memory_space=pltpu.VMEM)
    weights, member_coef, row_offsets = pl.pallas_call(
        functools.partial(window_kernel, n_grp, n_mem),
        out_shape=(
            jax.ShapeDtypeStruct((lines, LANES), f32),
            jax.ShapeDtypeStruct((MEM_DEV, inner), f32),
            jax.ShapeDtypeStruct((1, rows), f32),
        ),
        in_specs=[pl.BlockSpec(memory_space=pl.ANY)] * 8,
        out_specs=(whole,) * 3,
        scratch_shapes=[
            pltpu.VMEM((rows, width), bf16),
            pltpu.VMEM((rows, inner), bf16),
            pltpu.VMEM((1, rows), i32),
            pltpu.VMEM((1, rows), i32),
            pltpu.VMEM((1, rows), i32),
            pltpu.VMEM((1, rows), f32),
            held, held, held, held, held,
            pltpu.VMEM((1, rows), f32),
            pltpu.VMEM((calls, steps, lines, LANES), f32),
            pltpu.VMEM((calls, steps, lines, LANES), f32),
            pltpu.VMEM((slots, rows), bf16),
            pltpu.VMEM((n_mem - 1, cap, inner), bf16),
            pltpu.VMEM((slots, inner), bf16),
            pltpu.VMEM((slots, inner), bf16),
            pltpu.VMEM((inner, slots), bf16),
            pltpu.VMEM((n_mem - 1, 8, cap), f32),
            pltpu.VMEM((n_mem, 8, cap), f32),
            pltpu.VMEM((n_mem - 1, 8, cap), f32),
            pltpu.VMEM((n_mem, 8, cap), f32),
            pltpu.VMEM((MEM_DEV, inner, inner), f32),
            pltpu.VMEM((inner, slots), bf16),
            pltpu.VMEM((inner, slots), bf16),
            pltpu.VMEM((8, rows), f32),
            dma((7,)),
            dma((rows // 256,)),
            dma((calls, steps)),
            dma((calls, steps)),
            dma((n_mem - 1,)),
            dma((n_mem - 1,)),
            dma((n_mem - 1,)),
            dma((n_mem - 1,)),
            dma((n_mem - 1,)),
            dma((n_mem - 1,)),
        ],
        compiler_params=pltpu.CompilerParams(
            collective_id=0, has_side_effects=True, vmem_limit_bytes=60 << 20
        ),
        name="window",
    )(
        features,
        re_features,
        member_id.reshape(1, rows),
        slot.reshape(1, rows),
        labels.reshape(1, rows),
        offsets.reshape(1, rows),
        feature_scale.reshape(lines, LANES),
        w_start.reshape(lines, LANES),
    )
    return (weights.reshape(-1), member_coef, row_offsets.reshape(-1))


def solution(mesh):
    placed = (
        P(("grp", "mem"), None),
        P(("grp", "mem"), None),
        P(("grp", "mem")),
        P(("grp", "mem")),
        P(("grp", "mem")),
        P(("grp", "mem")),
        P(),
        P(),
    )
    return jax.shard_map(
        functools.partial(on_device, mesh.shape["grp"], mesh.shape["mem"]),
        mesh=mesh,
        in_specs=placed,
        out_specs=(P(), P(("grp", "mem"), None), P(("grp", "mem"))),
        check_vma=False,
    )
```

```python
import functools

import jax
import jax.numpy as jnp
from jax import lax
from jax.experimental import pallas as pl
from jax.experimental.pallas import tpu as pltpu
from jax.sharding import PartitionSpec as P

MEM_DEV = 8
NEWTON = 2
CG_ITERS = 3
LANES = 128
BLOCK = 32

ridge_fixed = 1.0
ridge_member = 1.0
MESH_ID = pl.DeviceIdType.MESH
NT = (((1,), (1,)), ((), ()))
NN = (((1,), (0,)), ((), ()))
TN = (((0,), (0,)), ((), ()))


def pair_rows(row):
    upper = row.astype(jnp.bfloat16).astype(jnp.float32)
    lower = (row - upper).astype(jnp.bfloat16).astype(jnp.float32)
    at = lax.broadcasted_iota(jnp.int32, (16, row.shape[1]), 0)
    both = jnp.where(at == 0, upper, jnp.where(at == 1, lower, 0.0))
    return both.astype(jnp.bfloat16)


def three_parts(value):
    first = value.astype(jnp.bfloat16)
    rest = value - first.astype(jnp.float32)
    second = rest.astype(jnp.bfloat16)
    third = (rest - second.astype(jnp.float32)).astype(jnp.bfloat16)
    return first, second, third


def invert_blocks(blocks):
    lane = lax.broadcasted_iota(jnp.int32, (BLOCK, LANES), 1)
    sub = lax.broadcasted_iota(jnp.int32, (BLOCK, LANES), 0)
    base = lane // BLOCK * BLOCK
    place = lane % BLOCK
    for k in range(0, BLOCK, 2):
        one, two = place == k, place == k + 1
        new = []
        for value in blocks:
            left = jnp.take_along_axis(value, base + k, axis=1)
            right = jnp.take_along_axis(value, base + k + 1, axis=1)
            a, b = left[k : k + 1, :], right[k : k + 1, :]
            c, d = left[k + 1 : k + 2, :], right[k + 1 : k + 2, :]
            inverse = 1.0 / (a * d - b * c)
            a, b, c, d = d * inverse, -b * inverse, -c * inverse, a * inverse
            top, low = value[k : k + 1, :], value[k + 1 : k + 2, :]
            at_one, at_two = one[0:1, :], two[0:1, :]
            first = jnp.where(at_one, a, jnp.where(at_two, b, a * top + b * low))
            second = jnp.where(at_one, c, jnp.where(at_two, d, c * top + d * low))
            value = jnp.where(one | two, 0.0, value) - left * first - right * second
            value = jnp.where(sub == k, first, jnp.where(sub == k + 1, second, value))
            new.append(value)
        blocks = new
    return blocks


def fit_members(z_ref, zt_ref, curv_row, resid_row, local, coef_ref, gram, upper, lower):
    width = z_ref.shape[1]
    slots = z_ref.shape[0]
    count = coef_ref.shape[0]
    per = LANES // BLOCK
    blocks = width // BLOCK
    weighted = zt_ref[...].astype(jnp.float32) * curv_row
    first = weighted.astype(jnp.bfloat16)
    upper[...] = first
    lower[...] = (weighted - first.astype(jnp.float32)).astype(jnp.bfloat16)
    eye = (
        lax.broadcasted_iota(jnp.int32, (width, width), 0)
        == lax.broadcasted_iota(jnp.int32, (width, width), 1)
    ).astype(jnp.float32)

    @pl.loop(0, count)
    def _(m):
        mask = jnp.where(local == m.astype(jnp.float32), 1.0, 0.0).astype(jnp.bfloat16)
        total = lax.dot_general(
            upper[...] * mask, z_ref[...], NN, preferred_element_type=jnp.float32
        ) + lax.dot_general(
            lower[...] * mask, z_ref[...], NN, preferred_element_type=jnp.float32
        )
        gram[m] = total + ridge_member * eye

    member = lax.broadcasted_iota(jnp.int32, (count, slots), 0).astype(jnp.float32)
    own = member == local
    masked = jnp.where(own, resid_row, 0.0)
    high = masked.astype(jnp.bfloat16)
    low = (masked - high.astype(jnp.float32)).astype(jnp.bfloat16)
    grad = lax.dot_general(
        high, z_ref[...], NN, preferred_element_type=jnp.float32
    ) + lax.dot_general(low, z_ref[...], NN, preferred_element_type=jnp.float32)
    rhs = [grad[m : m + 1, :] for m in range(count)]
    exact = dict(preferred_element_type=jnp.float32, precision=lax.Precision.HIGHEST)
    inverse_of = []
    heads = {}
    for b in range(blocks):
        lo, hi = b * BLOCK, (b + 1) * BLOCK
        squares = [gram[m, lo:hi, lo:hi] for m in range(count)]
        packed = [
            jnp.concatenate(squares[at : at + per], axis=1) for at in range(0, count, per)
        ]
        packed = invert_blocks(packed)
        inverses = [
            packed[m // per][:, m % per * BLOCK : (m % per + 1) * BLOCK] for m in range(count)
        ]
        panels = []
        if hi < width:
            for m in range(count):
                right = gram[m, lo:hi, hi:width]
                panel = lax.dot_general(inverses[m], right, NN, **exact)
                panels.append(panel)
                a1, a2, a3 = three_parts(right)
                b1, b2, b3 = three_parts(panel)
                left_cat = jnp.concatenate([a1, a1, a2, a2, a1, a3], axis=0)
                right_cat = jnp.concatenate([b1, b2, b1, b2, b3, b1], axis=0)
                gram[m, hi:width, hi:width] = gram[m, hi:width, hi:width] - lax.dot_general(
                    left_cat, right_cat, TN, preferred_element_type=jnp.float32
                )
                now = rhs[m]
                heads[(m, b)] = now[:, :BLOCK]
                rhs[m] = now[:, BLOCK:] - lax.dot_general(now[:, :BLOCK], panel, NN, **exact)
        else:
            for m in range(count):
                heads[(m, b)] = rhs[m]
        inverse_of.append((inverses, panels))
    solved = []
    for m in range(count):
        tail = None
        for b in reversed(range(blocks)):
            inverses, panels = inverse_of[b]
            part = lax.dot_general(heads[(m, b)], inverses[m], NN, **exact)
            if tail is not None:
                part = part - lax.dot_general(tail, panels[m], NT, **exact)
                tail = jnp.concatenate([part, tail], axis=1)
            else:
                tail = part
        solved.append(tail)
    coef = -jnp.concatenate(solved, axis=0)
    coef_ref[...] = coef
    high = coef.astype(jnp.bfloat16)
    low = (coef - high.astype(jnp.float32)).astype(jnp.bfloat16)
    scores = lax.dot_general(
        high, zt_ref[...], NN, preferred_element_type=jnp.float32
    ) + lax.dot_general(low, zt_ref[...], NN, preferred_element_type=jnp.float32)
    return jnp.sum(jnp.where(own, scores, 0.0), axis=0, keepdims=True)


def window_kernel(
    n_grp, n_mem,
    feat_hbm, re_hbm, member_hbm, slot_hbm, label_hbm, offset_hbm, scale_hbm, start_hbm,
    weight_ref, coef_ref, offsets_ref,
    feat, re_ref, member_ref, slot_ref, label_ref, offset_ref, scale_ref, vec_w,
    vec_u, vec_r, vec_p, curv, near_send, near_recv, far_send, far_recv,
    pick, z_send, z_ref, zs_ref, zt_ref, w_send, w_recv, s_send, s_recv, gram, upper, lower, row_vals,
    load_sem, feat_sem, ns_sem, nr_sem, fs_sem, fr_sem, zs_sem, zr_sem, ws_sem, wr_sem, ss_sem, sr_sem,
):
    rows, width = feat.shape
    lines = width // LANES
    slots = z_ref.shape[0]
    cap = slots // n_mem
    calls = NEWTON * (CG_ITERS + 1)
    each = n_mem // calls
    me_grp = lax.axis_index("grp")
    me_mem = lax.axis_index("mem")

    loads = [
        pltpu.make_async_copy(source, target, load_sem.at[i])
        for i, (source, target) in enumerate(
            (
                (scale_hbm, scale_ref), (start_hbm, vec_w), (offset_hbm, offset_ref),
                (label_hbm, label_ref), (slot_hbm, slot_ref), (member_hbm, member_ref),
                (re_hbm, re_ref),
            )
        )
    ]
    feat_loads = [
        pltpu.make_async_copy(
            feat_hbm.at[pl.ds(first, 256)], feat.at[pl.ds(first, 256)], feat_sem.at[first // 256]
        )
        for first in range(0, rows, 256)
    ]
    for load in loads[:4] + feat_loads + loads[4:]:
        load.start()

    low = 2
    high = n_mem // low
    near = n_grp * low
    me_low = lax.rem(me_mem, low)
    me_high = me_mem // low
    me_near = me_grp * low + me_low

    def near_peer(turn):
        other = lax.rem(me_near + turn, near)
        return (other // low, me_high * low + lax.rem(other, low))

    def far_peer(turn):
        return (me_grp, lax.rem(me_high + turn, high) * low + me_low)

    barrier = pltpu.get_barrier_semaphore()
    for turn in range(1, n_mem):
        pl.semaphore_signal(
            barrier, inc=1, device_id=(me_grp, lax.rem(me_mem + turn, n_mem)), device_id_type=MESH_ID
        )
    for turn in range(1, near):
        pl.semaphore_signal(barrier, inc=1, device_id=near_peer(turn), device_id_type=MESH_ID)
    pl.semaphore_wait(barrier, n_mem - 1 + near - 1)
    for load in loads[:4]:
        load.wait()

    def peer(turn):
        return (me_grp, lax.rem(me_mem + turn, n_mem))

    def z_copy(turn):
        return pltpu.make_async_remote_copy(
            src_ref=z_send.at[turn - 1],
            dst_ref=z_ref.at[pl.ds(pl.multiple_of(me_mem * cap, cap), cap)],
            send_sem=zs_sem.at[turn - 1],
            recv_sem=zr_sem.at[turn - 1],
            device_id=peer(turn),
            device_id_type=MESH_ID,
        )

    def build(turn):
        first = pl.multiple_of(lax.rem(me_mem + turn, n_mem) * cap, cap)
        at = lax.broadcasted_iota(jnp.int32, (cap, rows), 0) + first
        chosen = jnp.where(at == slot_ref[...], 1.0, 0.0).astype(jnp.bfloat16)
        pick[pl.ds(first, cap), :] = chosen
        block = lax.dot_general(chosen, re_ref[...], NN, preferred_element_type=jnp.float32)
        block = block.astype(jnp.bfloat16)

        @pl.when(turn < n_mem)
        def _():
            z_send[turn - 1] = block

        @pl.when(turn == n_mem)
        def _():
            z_ref[pl.ds(pl.multiple_of(me_mem * cap, cap), cap), :] = block

    def exchange(value, call, size, me, peer_of, source, slots_of, sends, recvs, between=None):
        source[call] = value
        copies = []
        for turn in range(1, size):
            copies.append(
                pltpu.make_async_remote_copy(
                    src_ref=source.at[call],
                    dst_ref=slots_of.at[call, me],
                    send_sem=sends.at[call, turn - 1],
                    recv_sem=recvs.at[call, turn - 1],
                    device_id=peer_of(turn),
                    device_id_type=MESH_ID,
                )
            )
        for copy in copies:
            copy.start()
        slots_of[call, me] = value
        if between is not None:
            between()
        for copy in copies:
            copy.wait()
        parts = [slots_of[call, i] for i in range(size)]
        while len(parts) > 1:
            parts = [parts[i] + parts[i + 1] for i in range(0, len(parts), 2)]
        return parts[0]

    def all_sum(value, call):
        def fill():
            for q in range(each):
                build(1 + call * each + q)

        value = exchange(
            value, call, near, me_near, near_peer, near_send, near_recv, ns_sem, nr_sem, fill
        )
        value = exchange(
            value, call, high, me_high, far_peer, far_send, far_recv, fs_sem, fr_sem
        )
        for q in range(each):
            turn = 1 + call * each + q

            @pl.when(turn < n_mem)
            def _():
                z_copy(turn).start()

        return value

    def times_rows(vector, loading=None):
        row = jnp.concatenate([vector[i : i + 1, :] for i in range(lines)], axis=1)
        pair = pair_rows(row)
        parts = []
        for first in range(0, rows, 256):
            if loading is not None:
                @pl.when(loading == 0)
                def _():
                    feat_loads[first // 256].wait()
            got = lax.dot_general(
                pair, feat[first : first + 256, :], NT, preferred_element_type=jnp.float32
            )
            parts.append(got[0:1] + got[1:2])
        return jnp.concatenate(parts, axis=1)

    def times_columns(row):
        pair = pair_rows(row)
        parts = []
        for first in range(0, width, 256):
            got = lax.dot_general(
                pair, feat[:, first : first + 256], NN, preferred_element_type=jnp.float32
            )
            got = got[0:1] + got[1:2]
            parts += [got[:, at : at + LANES] for at in range(0, 256, LANES)]
        return jnp.concatenate(parts, axis=0)

    def total(value):
        return jnp.sum(jnp.sum(value, axis=1, keepdims=True), axis=0, keepdims=True)

    scale = scale_ref[...]
    target = label_ref[...].astype(jnp.float32)

    def newton(step, carry):
        base = step * (CG_ITERS + 1)
        weights = vec_w[...]
        margin = times_rows(scale * weights, step) + offset_ref[...]
        prob = 1.0 / (1.0 + jnp.exp(-margin))
        curv[...] = prob * (1.0 - prob)
        grad = times_columns(prob - target)

        @pl.when(step == 0)
        def _():
            for load in loads[4:]:
                load.wait()

        summed = all_sum(grad, base)
        resid = -(scale * summed + ridge_fixed * weights)
        vec_r[...] = resid
        vec_p[...] = resid
        vec_u[...] = jnp.zeros_like(resid)

        def cg(k, norm):
            direction = vec_p[...]
            inner = curv[...] * times_rows(scale * direction)
            image = scale * all_sum(times_columns(inner), base + 1 + k) + ridge_fixed * direction
            size = norm / total(direction * image)
            vec_u[...] = vec_u[...] + size * direction
            left = vec_r[...] - size * image
            vec_r[...] = left
            new_norm = total(left * left)
            vec_p[...] = left + new_norm / norm * direction
            return new_norm

        lax.fori_loop(0, CG_ITERS, cg, total(resid * resid))
        vec_w[...] = weights + vec_u[...]
        return carry

    lax.fori_loop(0, NEWTON, newton, 0)
    weights = vec_w[...]
    weight_ref[...] = weights
    score = times_rows(scale * weights)
    prob = 1.0 / (1.0 + jnp.exp(-score))
    local_id = lax.rem(member_ref[...], MEM_DEV).astype(jnp.float32)
    row_vals[...] = jnp.zeros_like(row_vals)
    row_vals[0:1, :] = prob * (1.0 - prob)
    row_vals[1:2, :] = prob - target
    row_vals[2:3, :] = local_id
    parts = jnp.concatenate([p.astype(jnp.float32) for p in three_parts(row_vals[...])], axis=0)
    parts = jnp.concatenate([parts, jnp.zeros_like(parts[0:8])], axis=0).astype(jnp.bfloat16)

    def small_copy(source, target, turn, sends, recvs):
        return pltpu.make_async_remote_copy(
            src_ref=source.at[turn - 1],
            dst_ref=target.at[turn - 1],
            send_sem=sends.at[turn - 1],
            recv_sem=recvs.at[turn - 1],
            device_id=peer(turn),
            device_id_type=MESH_ID,
        )

    for turn in range(1, n_mem + 1):
        first = pl.multiple_of(lax.rem(me_mem + turn, n_mem) * cap, cap)
        got = lax.dot_general(
            parts, pick[pl.ds(first, cap), :], NT, preferred_element_type=jnp.float32
        )
        got = got[0:8] + got[8:16] + got[16:24]
        if turn < n_mem:
            w_send[turn - 1] = got
            small_copy(w_send, w_recv, turn, ws_sem, wr_sem).start()
        else:
            w_recv[n_mem - 1] = got
    for turn in range(1, n_mem):
        z_copy(turn).wait()
    for turn in range(1, n_mem + 1):
        source = lax.rem(me_mem + n_mem - turn, n_mem)
        block = z_ref[pl.ds(pl.multiple_of(source * cap, cap), cap), :]
        zt_ref[:, (turn - 1) * cap : turn * cap] = block.T
        zs_ref[(turn - 1) * cap : turn * cap, :] = block
    for turn in range(1, n_mem):
        small_copy(w_send, w_recv, turn, ws_sem, wr_sem).wait()
    arrived = jnp.concatenate([w_recv[t] for t in range(n_mem)], axis=1)
    scores = fit_members(
        zs_ref, zt_ref, arrived[0:1], arrived[1:2], arrived[2:3], coef_ref, gram, upper, lower
    )
    for turn in range(1, n_mem + 1):
        back = jnp.broadcast_to(scores[:, (turn - 1) * cap : turn * cap], (8, cap))
        if turn < n_mem:
            s_send[n_mem - turn - 1] = back
        else:
            s_recv[n_mem - 1] = back
    for turn in range(1, n_mem):
        small_copy(s_send, s_recv, turn, ss_sem, sr_sem).start()
    for turn in range(1, n_mem):
        small_copy(s_send, s_recv, turn, ss_sem, sr_sem).wait()
    result = jnp.zeros((1, rows), jnp.float32)
    for turn in range(1, n_mem + 1):
        owner = lax.rem(me_mem + n_mem - turn, n_mem)
        value = s_recv[turn - 1][0:1]
        p1, p2, p3 = (p.astype(jnp.float32) for p in three_parts(value))
        at = lax.broadcasted_iota(jnp.int32, (16, cap), 0)
        stack = jnp.where(at == 0, p1, jnp.where(at == 1, p2, jnp.where(at == 2, p3, 0.0)))
        got = lax.dot_general(
            stack.astype(jnp.bfloat16),
            pick[pl.ds(pl.multiple_of(owner * cap, cap), cap), :],
            NN,
            preferred_element_type=jnp.float32,
        )
        result = result + (got[0:1] + got[1:2] + got[2:3])
    offsets_ref[...] = result


def on_device(n_grp, n_mem, features, re_features, member_id, slot, labels, offsets, feature_scale, w_start):
    rows, width = features.shape
    inner = re_features.shape[1]
    lines = width // LANES
    slots = 2 * rows
    cap = slots // n_mem
    near, high = 2 * n_grp, n_mem // 2
    calls = NEWTON * (CG_ITERS + 1)
    f32, bf16, i32 = jnp.float32, jnp.bfloat16, jnp.int32
    held = pltpu.VMEM((lines, LANES), f32)
    dma = pltpu.SemaphoreType.DMA
    whole = pl.BlockSpec(memory_space=pltpu.VMEM)
    weights, member_coef, row_offsets = pl.pallas_call(
        functools.partial(window_kernel, n_grp, n_mem),
        out_shape=(
            jax.ShapeDtypeStruct((lines, LANES), f32),
            jax.ShapeDtypeStruct((MEM_DEV, inner), f32),
            jax.ShapeDtypeStruct((1, rows), f32),
        ),
        in_specs=[pl.BlockSpec(memory_space=pl.ANY)] * 8,
        out_specs=(whole,) * 3,
        scratch_shapes=[
            pltpu.VMEM((rows, width), bf16),
            pltpu.VMEM((rows, inner), bf16),
            pltpu.VMEM((1, rows), i32),
            pltpu.VMEM((1, rows), i32),
            pltpu.VMEM((1, rows), i32),
            pltpu.VMEM((1, rows), f32),
            held, held, held, held, held,
            pltpu.VMEM((1, rows), f32),
            pltpu.VMEM((calls, lines, LANES), f32),
            pltpu.VMEM((calls, near, lines, LANES), f32),
            pltpu.VMEM((calls, lines, LANES), f32),
            pltpu.VMEM((calls, high, lines, LANES), f32),
            pltpu.VMEM((slots, rows), bf16),
            pltpu.VMEM((n_mem - 1, cap, inner), bf16),
            pltpu.VMEM((slots, inner), bf16),
            pltpu.VMEM((slots, inner), bf16),
            pltpu.VMEM((inner, slots), bf16),
            pltpu.VMEM((n_mem - 1, 8, cap), f32),
            pltpu.VMEM((n_mem, 8, cap), f32),
            pltpu.VMEM((n_mem - 1, 8, cap), f32),
            pltpu.VMEM((n_mem, 8, cap), f32),
            pltpu.VMEM((MEM_DEV, inner, inner), f32),
            pltpu.VMEM((inner, slots), bf16),
            pltpu.VMEM((inner, slots), bf16),
            pltpu.VMEM((8, rows), f32),
            dma((7,)),
            dma((rows // 256,)),
            dma((calls, near - 1)),
            dma((calls, near - 1)),
            dma((calls, high - 1)),
            dma((calls, high - 1)),
            dma((n_mem - 1,)),
            dma((n_mem - 1,)),
            dma((n_mem - 1,)),
            dma((n_mem - 1,)),
            dma((n_mem - 1,)),
            dma((n_mem - 1,)),
        ],
        compiler_params=pltpu.CompilerParams(
            collective_id=0, has_side_effects=True, vmem_limit_bytes=60 << 20
        ),
        name="window",
    )(
        features,
        re_features,
        member_id.reshape(1, rows),
        slot.reshape(1, rows),
        labels.reshape(1, rows),
        offsets.reshape(1, rows),
        feature_scale.reshape(lines, LANES),
        w_start.reshape(lines, LANES),
    )
    return (weights.reshape(-1), member_coef, row_offsets.reshape(-1))


def solution(mesh):
    placed = (
        P(("grp", "mem"), None),
        P(("grp", "mem"), None),
        P(("grp", "mem")),
        P(("grp", "mem")),
        P(("grp", "mem")),
        P(("grp", "mem")),
        P(),
        P(),
    )
    return jax.shard_map(
        functools.partial(on_device, mesh.shape["grp"], mesh.shape["mem"]),
        mesh=mesh,
        in_specs=placed,
        out_specs=(P(), P(("grp", "mem"), None), P(("grp", "mem"))),
        check_vma=False,
    )
```

```python
import functools

import jax
import jax.numpy as jnp
from jax import lax
from jax.experimental import pallas as pl
from jax.experimental.pallas import tpu as pltpu
from jax.sharding import PartitionSpec as P

MEM_DEV = 8
NEWTON = 2
CG_ITERS = 3
LANES = 128
BLOCK = 32

ridge_fixed = 1.0
ridge_member = 1.0
MESH_ID = pl.DeviceIdType.MESH
NT = (((1,), (1,)), ((), ()))
NN = (((1,), (0,)), ((), ()))
TN = (((0,), (0,)), ((), ()))


def pair_rows(row):
    upper = row.astype(jnp.bfloat16).astype(jnp.float32)
    lower = (row - upper).astype(jnp.bfloat16).astype(jnp.float32)
    at = lax.broadcasted_iota(jnp.int32, (16, row.shape[1]), 0)
    both = jnp.where(at == 0, upper, jnp.where(at == 1, lower, 0.0))
    return both.astype(jnp.bfloat16)


def three_parts(value):
    first = value.astype(jnp.bfloat16)
    rest = value - first.astype(jnp.float32)
    second = rest.astype(jnp.bfloat16)
    third = (rest - second.astype(jnp.float32)).astype(jnp.bfloat16)
    return first, second, third


def invert_blocks(blocks):
    lane = lax.broadcasted_iota(jnp.int32, (BLOCK, LANES), 1)
    sub = lax.broadcasted_iota(jnp.int32, (BLOCK, LANES), 0)
    base = lane // BLOCK * BLOCK
    place = lane % BLOCK
    for k in range(0, BLOCK, 2):
        one, two = place == k, place == k + 1
        new = []
        for value in blocks:
            left = jnp.take_along_axis(value, base + k, axis=1)
            right = jnp.take_along_axis(value, base + k + 1, axis=1)
            a, b = left[k : k + 1, :], right[k : k + 1, :]
            c, d = left[k + 1 : k + 2, :], right[k + 1 : k + 2, :]
            inverse = 1.0 / (a * d - b * c)
            a, b, c, d = d * inverse, -b * inverse, -c * inverse, a * inverse
            top, low = value[k : k + 1, :], value[k + 1 : k + 2, :]
            at_one, at_two = one[0:1, :], two[0:1, :]
            first = jnp.where(at_one, a, jnp.where(at_two, b, a * top + b * low))
            second = jnp.where(at_one, c, jnp.where(at_two, d, c * top + d * low))
            value = jnp.where(one | two, 0.0, value) - left * first - right * second
            value = jnp.where(sub == k, first, jnp.where(sub == k + 1, second, value))
            new.append(value)
        blocks = new
        yield blocks


def fit_members(z_ref, zt_ref, curv_row, resid_row, local, coef_ref, gram, upper, lower):
    width = z_ref.shape[1]
    slots = z_ref.shape[0]
    count = coef_ref.shape[0]
    per = LANES // BLOCK
    blocks = width // BLOCK
    weighted = zt_ref[...].astype(jnp.float32) * curv_row
    first = weighted.astype(jnp.bfloat16)
    upper[...] = first
    lower[...] = (weighted - first.astype(jnp.float32)).astype(jnp.bfloat16)
    eye = (
        lax.broadcasted_iota(jnp.int32, (width, width), 0)
        == lax.broadcasted_iota(jnp.int32, (width, width), 1)
    ).astype(jnp.float32)

    @pl.loop(0, count)
    def _(m):
        mask = jnp.where(local == m.astype(jnp.float32), 1.0, 0.0).astype(jnp.bfloat16)
        total = lax.dot_general(
            upper[...] * mask, z_ref[...], NN, preferred_element_type=jnp.float32
        ) + lax.dot_general(
            lower[...] * mask, z_ref[...], NN, preferred_element_type=jnp.float32
        )
        gram[m] = total + ridge_member * eye

    member = lax.broadcasted_iota(jnp.int32, (count, slots), 0).astype(jnp.float32)
    own = member == local
    masked = jnp.where(own, resid_row, 0.0)
    high = masked.astype(jnp.bfloat16)
    low = (masked - high.astype(jnp.float32)).astype(jnp.bfloat16)
    grad = lax.dot_general(
        high, z_ref[...], NN, preferred_element_type=jnp.float32
    ) + lax.dot_general(low, z_ref[...], NN, preferred_element_type=jnp.float32)
    rhs = [grad[m : m + 1, :] for m in range(count)]
    exact = dict(preferred_element_type=jnp.float32, precision=lax.Precision.HIGHEST)
    inverse_of = []
    heads = {}
    rows_now = [gram[m, 0:BLOCK, :] for m in range(count)]
    start = 0
    later = []

    def trailing(m, first, start, left_cat, right_cat):
        update = lax.dot_general(left_cat, right_cat, TN, preferred_element_type=jnp.float32)
        gram[m, first:width, start:width] = gram[m, first:width, start:width] - update[first - start :]

    for b in range(blocks):
        lo, hi = b * BLOCK, (b + 1) * BLOCK
        squares = [rows_now[m][:, lo - start : hi - start] for m in range(count)]
        packed = [
            jnp.concatenate(squares[at : at + per], axis=1) for at in range(0, count, per)
        ]
        for step, packed in enumerate(invert_blocks(packed)):
            if later and step % 2 == 1:
                later.pop(0)()
        while later:
            later.pop(0)()
        inverses = [
            packed[m // per][:, m % per * BLOCK : (m % per + 1) * BLOCK] for m in range(count)
        ]
        panels = []
        following = []
        new_start = hi // LANES * LANES
        for m in range(count):
            head = rhs[m][:, lo - start : hi - start]
            heads[(m, b)] = head
            if hi == width:
                continue
            right = rows_now[m][:, new_start - start :]
            panel = lax.dot_general(inverses[m], right, NN, **exact)
            panels.append(panel)
            a1, a2, a3 = three_parts(right)
            b1, b2, b3 = three_parts(panel)
            left_cat = jnp.concatenate([a1, a1, a2, a2, a1, a3], axis=0)
            right_cat = jnp.concatenate([b1, b2, b1, b2, b3, b1], axis=0)
            skip = hi - new_start
            following.append(
                gram[m, hi : hi + BLOCK, new_start:width]
                - lax.dot_general(
                    left_cat[:, skip : skip + BLOCK],
                    right_cat,
                    TN,
                    preferred_element_type=jnp.float32,
                )
            )
            if hi + BLOCK < width:
                later.append(
                    functools.partial(trailing, m, hi + BLOCK, new_start, left_cat, right_cat)
                )
            rhs[m] = rhs[m][:, new_start - start :] - lax.dot_general(head, panel, NN, **exact)
        rows_now = following
        inverse_of.append((inverses, panels, new_start))
        start = new_start
    pieces = [[None] * blocks for _ in range(count)]
    for b in reversed(range(blocks)):
        inverses, panels, begin = inverse_of[b]
        for m in range(count):
            part = lax.dot_general(heads[(m, b)], inverses[m], NN, **exact)
            if panels:
                gap = (b + 1) * BLOCK - begin
                tail = ([jnp.zeros((1, gap), jnp.float32)] if gap else []) + pieces[m][b + 1 :]
                tail = jnp.concatenate(tail, axis=1) if len(tail) > 1 else tail[0]
                part = part - lax.dot_general(tail, panels[m], NT, **exact)
            pieces[m][b] = part
    solved = [jnp.concatenate(pieces[m], axis=1) for m in range(count)]
    coef = -jnp.concatenate(solved, axis=0)
    coef_ref[...] = coef
    high = coef.astype(jnp.bfloat16)
    low = (coef - high.astype(jnp.float32)).astype(jnp.bfloat16)
    scores = lax.dot_general(
        high, zt_ref[...], NN, preferred_element_type=jnp.float32
    ) + lax.dot_general(low, zt_ref[...], NN, preferred_element_type=jnp.float32)
    return jnp.sum(jnp.where(own, scores, 0.0), axis=0, keepdims=True)


def window_kernel(
    n_grp, n_mem,
    feat_hbm, re_hbm, member_hbm, slot_hbm, label_hbm, offset_hbm, scale_hbm, start_hbm,
    weight_ref, coef_ref, offsets_ref,
    feat, re_ref, member_ref, slot_ref, label_ref, offset_ref, scale_ref, vec_w,
    vec_u, vec_r, vec_p, curv, near_send, near_recv, far_send, far_recv,
    pick, z_send, z_ref, zs_ref, zt_ref, w_send, w_recv, s_send, s_recv, gram, upper, lower, row_vals,
    load_sem, feat_sem, ns_sem, nr_sem, fs_sem, fr_sem, zs_sem, zr_sem, ws_sem, wr_sem, ss_sem, sr_sem,
):
    rows, width = feat.shape
    lines = width // LANES
    slots = z_ref.shape[0]
    cap = slots // n_mem
    calls = NEWTON * (CG_ITERS + 1)
    each = n_mem // calls
    me_grp = lax.axis_index("grp")
    me_mem = lax.axis_index("mem")

    loads = [
        pltpu.make_async_copy(source, target, load_sem.at[i])
        for i, (source, target) in enumerate(
            (
                (scale_hbm, scale_ref), (start_hbm, vec_w), (offset_hbm, offset_ref),
                (label_hbm, label_ref), (slot_hbm, slot_ref), (member_hbm, member_ref),
                (re_hbm, re_ref),
            )
        )
    ]
    feat_loads = [
        pltpu.make_async_copy(
            feat_hbm.at[pl.ds(first, 256)], feat.at[pl.ds(first, 256)], feat_sem.at[first // 256]
        )
        for first in range(0, rows, 256)
    ]
    for load in loads[:4] + feat_loads + loads[4:]:
        load.start()

    low = 2
    high = n_mem // low
    near = n_grp * low
    me_low = lax.rem(me_mem, low)
    me_high = me_mem // low
    me_near = me_grp * low + me_low

    def near_peer(turn):
        other = lax.rem(me_near + turn, near)
        return (other // low, me_high * low + lax.rem(other, low))

    def far_peer(turn):
        return (me_grp, lax.rem(me_high + turn, high) * low + me_low)

    barrier = pltpu.get_barrier_semaphore()
    for turn in range(1, n_mem):
        pl.semaphore_signal(
            barrier, inc=1, device_id=(me_grp, lax.rem(me_mem + turn, n_mem)), device_id_type=MESH_ID
        )
    for turn in range(1, near):
        pl.semaphore_signal(barrier, inc=1, device_id=near_peer(turn), device_id_type=MESH_ID)
    pl.semaphore_wait(barrier, n_mem - 1 + near - 1)
    for load in loads[:4]:
        load.wait()

    def peer(turn):
        return (me_grp, lax.rem(me_mem + turn, n_mem))

    def z_copy(turn):
        return pltpu.make_async_remote_copy(
            src_ref=z_send.at[turn - 1],
            dst_ref=z_ref.at[pl.ds(pl.multiple_of(me_mem * cap, cap), cap)],
            send_sem=zs_sem.at[turn - 1],
            recv_sem=zr_sem.at[turn - 1],
            device_id=peer(turn),
            device_id_type=MESH_ID,
        )

    def build(turn):
        first = pl.multiple_of(lax.rem(me_mem + turn, n_mem) * cap, cap)
        at = lax.broadcasted_iota(jnp.int32, (cap, rows), 0) + first
        chosen = jnp.where(at == slot_ref[...], 1.0, 0.0).astype(jnp.bfloat16)
        pick[pl.ds(first, cap), :] = chosen
        block = lax.dot_general(chosen, re_ref[...], NN, preferred_element_type=jnp.float32)
        block = block.astype(jnp.bfloat16)

        @pl.when(turn < n_mem)
        def _():
            z_send[turn - 1] = block

        @pl.when(turn == n_mem)
        def _():
            z_ref[pl.ds(pl.multiple_of(me_mem * cap, cap), cap), :] = block

    def exchange(value, call, size, me, peer_of, source, slots_of, sends, recvs, between=None):
        source[call] = value
        copies = []
        for turn in range(1, size):
            copies.append(
                pltpu.make_async_remote_copy(
                    src_ref=source.at[call],
                    dst_ref=slots_of.at[call, me],
                    send_sem=sends.at[call, turn - 1],
                    recv_sem=recvs.at[call, turn - 1],
                    device_id=peer_of(turn),
                    device_id_type=MESH_ID,
                )
            )
        for copy in copies:
            copy.start()
        slots_of[call, me] = value
        if between is not None:
            between()
        for copy in copies:
            copy.wait()
        parts = [slots_of[call, i] for i in range(size)]
        while len(parts) > 1:
            parts = [parts[i] + parts[i + 1] for i in range(0, len(parts), 2)]
        return parts[0]

    def all_sum(value, call):
        def fill():
            for q in range(each):
                build(1 + call * each + q)

        value = exchange(
            value, call, near, me_near, near_peer, near_send, near_recv, ns_sem, nr_sem, fill
        )
        value = exchange(
            value, call, high, me_high, far_peer, far_send, far_recv, fs_sem, fr_sem
        )
        for q in range(each):
            turn = 1 + call * each + q

            @pl.when(turn < n_mem)
            def _():
                z_copy(turn).start()

        return value

    def times_rows(vector, loading=None):
        row = jnp.concatenate([vector[i : i + 1, :] for i in range(lines)], axis=1)
        pair = pair_rows(row)
        parts = []
        for first in range(0, rows, 256):
            if loading is not None:
                @pl.when(loading == 0)
                def _():
                    feat_loads[first // 256].wait()
            got = lax.dot_general(
                pair, feat[first : first + 256, :], NT, preferred_element_type=jnp.float32
            )
            parts.append(got[0:1] + got[1:2])
        return jnp.concatenate(parts, axis=1)

    def times_columns(row):
        pair = pair_rows(row)
        parts = []
        for first in range(0, width, 256):
            got = lax.dot_general(
                pair, feat[:, first : first + 256], NN, preferred_element_type=jnp.float32
            )
            got = got[0:1] + got[1:2]
            parts += [got[:, at : at + LANES] for at in range(0, 256, LANES)]
        return jnp.concatenate(parts, axis=0)

    def total(value):
        return jnp.sum(jnp.sum(value, axis=1, keepdims=True), axis=0, keepdims=True)

    scale = scale_ref[...]
    target = label_ref[...].astype(jnp.float32)

    def newton(step, carry):
        base = step * (CG_ITERS + 1)
        weights = vec_w[...]
        margin = times_rows(scale * weights, step) + offset_ref[...]
        prob = 1.0 / (1.0 + jnp.exp(-margin))
        curv[...] = prob * (1.0 - prob)
        grad = times_columns(prob - target)

        @pl.when(step == 0)
        def _():
            for load in loads[4:]:
                load.wait()

        summed = all_sum(grad, base)
        resid = -(scale * summed + ridge_fixed * weights)
        vec_r[...] = resid
        vec_p[...] = resid
        vec_u[...] = jnp.zeros_like(resid)

        def cg(k, norm):
            direction = vec_p[...]
            inner = curv[...] * times_rows(scale * direction)
            image = scale * all_sum(times_columns(inner), base + 1 + k) + ridge_fixed * direction
            size = norm / total(direction * image)
            vec_u[...] = vec_u[...] + size * direction
            left = vec_r[...] - size * image
            vec_r[...] = left
            new_norm = total(left * left)
            vec_p[...] = left + new_norm / norm * direction
            return new_norm

        lax.fori_loop(0, CG_ITERS, cg, total(resid * resid))
        vec_w[...] = weights + vec_u[...]
        return carry

    lax.fori_loop(0, NEWTON, newton, 0)
    weights = vec_w[...]
    weight_ref[...] = weights
    score = times_rows(scale * weights)
    prob = 1.0 / (1.0 + jnp.exp(-score))
    local_id = lax.rem(member_ref[...], MEM_DEV).astype(jnp.float32)
    row_vals[...] = jnp.zeros_like(row_vals)
    row_vals[0:1, :] = prob * (1.0 - prob)
    row_vals[1:2, :] = prob - target
    row_vals[2:3, :] = local_id
    parts = jnp.concatenate([p.astype(jnp.float32) for p in three_parts(row_vals[...])], axis=0)
    parts = jnp.concatenate([parts, jnp.zeros_like(parts[0:8])], axis=0).astype(jnp.bfloat16)

    def small_copy(source, target, turn, sends, recvs):
        return pltpu.make_async_remote_copy(
            src_ref=source.at[turn - 1],
            dst_ref=target.at[turn - 1],
            send_sem=sends.at[turn - 1],
            recv_sem=recvs.at[turn - 1],
            device_id=peer(turn),
            device_id_type=MESH_ID,
        )

    for turn in range(1, n_mem + 1):
        first = pl.multiple_of(lax.rem(me_mem + turn, n_mem) * cap, cap)
        got = lax.dot_general(
            parts, pick[pl.ds(first, cap), :], NT, preferred_element_type=jnp.float32
        )
        got = got[0:8] + got[8:16] + got[16:24]
        if turn < n_mem:
            w_send[turn - 1] = got
            small_copy(w_send, w_recv, turn, ws_sem, wr_sem).start()
        else:
            w_recv[n_mem - 1] = got
    for turn in range(1, n_mem):
        z_copy(turn).wait()
    for turn in range(1, n_mem + 1):
        source = lax.rem(me_mem + n_mem - turn, n_mem)
        block = z_ref[pl.ds(pl.multiple_of(source * cap, cap), cap), :]
        zt_ref[:, (turn - 1) * cap : turn * cap] = block.T
        zs_ref[(turn - 1) * cap : turn * cap, :] = block
    for turn in range(1, n_mem):
        small_copy(w_send, w_recv, turn, ws_sem, wr_sem).wait()
    arrived = jnp.concatenate([w_recv[t] for t in range(n_mem)], axis=1)
    scores = fit_members(
        zs_ref, zt_ref, arrived[0:1], arrived[1:2], arrived[2:3], coef_ref, gram, upper, lower
    )
    for turn in range(1, n_mem + 1):
        back = jnp.broadcast_to(scores[:, (turn - 1) * cap : turn * cap], (8, cap))
        if turn < n_mem:
            s_send[n_mem - turn - 1] = back
        else:
            s_recv[n_mem - 1] = back
    for turn in range(1, n_mem):
        small_copy(s_send, s_recv, turn, ss_sem, sr_sem).start()
    for turn in range(1, n_mem):
        small_copy(s_send, s_recv, turn, ss_sem, sr_sem).wait()
    result = jnp.zeros((1, rows), jnp.float32)
    for turn in range(1, n_mem + 1):
        owner = lax.rem(me_mem + n_mem - turn, n_mem)
        value = s_recv[turn - 1][0:1]
        p1, p2, p3 = (p.astype(jnp.float32) for p in three_parts(value))
        at = lax.broadcasted_iota(jnp.int32, (16, cap), 0)
        stack = jnp.where(at == 0, p1, jnp.where(at == 1, p2, jnp.where(at == 2, p3, 0.0)))
        got = lax.dot_general(
            stack.astype(jnp.bfloat16),
            pick[pl.ds(pl.multiple_of(owner * cap, cap), cap), :],
            NN,
            preferred_element_type=jnp.float32,
        )
        result = result + (got[0:1] + got[1:2] + got[2:3])
    offsets_ref[...] = result


def on_device(n_grp, n_mem, features, re_features, member_id, slot, labels, offsets, feature_scale, w_start):
    rows, width = features.shape
    inner = re_features.shape[1]
    lines = width // LANES
    slots = 2 * rows
    cap = slots // n_mem
    near, high = 2 * n_grp, n_mem // 2
    calls = NEWTON * (CG_ITERS + 1)
    f32, bf16, i32 = jnp.float32, jnp.bfloat16, jnp.int32
    held = pltpu.VMEM((lines, LANES), f32)
    dma = pltpu.SemaphoreType.DMA
    whole = pl.BlockSpec(memory_space=pltpu.VMEM)
    weights, member_coef, row_offsets = pl.pallas_call(
        functools.partial(window_kernel, n_grp, n_mem),
        out_shape=(
            jax.ShapeDtypeStruct((lines, LANES), f32),
            jax.ShapeDtypeStruct((MEM_DEV, inner), f32),
            jax.ShapeDtypeStruct((1, rows), f32),
        ),
        in_specs=[pl.BlockSpec(memory_space=pl.ANY)] * 8,
        out_specs=(whole,) * 3,
        scratch_shapes=[
            pltpu.VMEM((rows, width), bf16),
            pltpu.VMEM((rows, inner), bf16),
            pltpu.VMEM((1, rows), i32),
            pltpu.VMEM((1, rows), i32),
            pltpu.VMEM((1, rows), i32),
            pltpu.VMEM((1, rows), f32),
            held, held, held, held, held,
            pltpu.VMEM((1, rows), f32),
            pltpu.VMEM((calls, lines, LANES), f32),
            pltpu.VMEM((calls, near, lines, LANES), f32),
            pltpu.VMEM((calls, lines, LANES), f32),
            pltpu.VMEM((calls, high, lines, LANES), f32),
            pltpu.VMEM((slots, rows), bf16),
            pltpu.VMEM((n_mem - 1, cap, inner), bf16),
            pltpu.VMEM((slots, inner), bf16),
            pltpu.VMEM((slots, inner), bf16),
            pltpu.VMEM((inner, slots), bf16),
            pltpu.VMEM((n_mem - 1, 8, cap), f32),
            pltpu.VMEM((n_mem, 8, cap), f32),
            pltpu.VMEM((n_mem - 1, 8, cap), f32),
            pltpu.VMEM((n_mem, 8, cap), f32),
            pltpu.VMEM((MEM_DEV, inner, inner), f32),
            pltpu.VMEM((inner, slots), bf16),
            pltpu.VMEM((inner, slots), bf16),
            pltpu.VMEM((8, rows), f32),
            dma((7,)),
            dma((rows // 256,)),
            dma((calls, near - 1)),
            dma((calls, near - 1)),
            dma((calls, high - 1)),
            dma((calls, high - 1)),
            dma((n_mem - 1,)),
            dma((n_mem - 1,)),
            dma((n_mem - 1,)),
            dma((n_mem - 1,)),
            dma((n_mem - 1,)),
            dma((n_mem - 1,)),
        ],
        compiler_params=pltpu.CompilerParams(
            collective_id=0, has_side_effects=True, vmem_limit_bytes=60 << 20
        ),
        name="window",
    )(
        features,
        re_features,
        member_id.reshape(1, rows),
        slot.reshape(1, rows),
        labels.reshape(1, rows),
        offsets.reshape(1, rows),
        feature_scale.reshape(lines, LANES),
        w_start.reshape(lines, LANES),
    )
    return (weights.reshape(-1), member_coef, row_offsets.reshape(-1))


def solution(mesh):
    placed = (
        P(("grp", "mem"), None),
        P(("grp", "mem"), None),
        P(("grp", "mem")),
        P(("grp", "mem")),
        P(("grp", "mem")),
        P(("grp", "mem")),
        P(),
        P(),
    )
    return jax.shard_map(
        functools.partial(on_device, mesh.shape["grp"], mesh.shape["mem"]),
        mesh=mesh,
        in_specs=placed,
        out_specs=(P(), P(("grp", "mem"), None), P(("grp", "mem"))),
        check_vma=False,
    )
```
